32 devices in a mesh: req: 16 (over z, y, x), tp: 2 (over core).
Axes of the slice: x: 2, y: 2, z: 4, core: 2. Of those that a mesh axis runs over, the one named last changes fastest.
Arguments:
- tokens: bfloat16 [8192, 3072], P('req', 'tp'), may hold values from -6 to 6
- norm_gain: bfloat16 [3072], P('tp'), may hold values from 0.099609375 to 1.8984375
- qkv_weight: bfloat16 [3, 3072, 3072], P(None, 'req', 'tp'), may hold values from -0.109375 to 0.109375
- out_weight: bfloat16 [3072, 3072], P('tp', 'req'), may hold values from -1.75 to 1.75
- cache: bfloat16 [16, 2, 2048, 3072], P('req', None, None, 'tp'), may hold values from -720 to 720
- cache_lens: int32 [16], P('req'), may hold values from 0 to 2048, as said below
- valid_tokens: int32 [16], P('req'), may hold values from 128 to 512, as said below
Outputs:
- mixed: bfloat16 [8192, 3072], P('req', 'tp')
- new_entries: bfloat16 [16, 2, 512, 3072], P('req', None, None, 'tp')
The draws below stay inside these ranges and needn't reach their ends.
Inputs may be any that keep to these rules, and one draw needn't show every extreme that they name: `cache_lens`: in every draw some request's cache holds all 2048 entries and some request's cache is empty. `valid_tokens`: in every draw some request brings 512 live new tokens.
All inputs are finite; a program needn't handle non-finite values.
Results may differ from the reference program's by a relative error of at most 0.0095.
The reference program's roundings to bfloat16 on the way count: a program that leaves them out, or rounds other values in their place, can miss the bound.
Values may be sent and summed in bfloat16 or wider, within the bound.
A program may use at most 192 MiB of HBM per device.

```python
import math
import jax
import jax.numpy as jnp
from jax import lax

D = 3072
HEADS = 32
HD = 96
SPAN = 512
CACHE = 2048
REQS = 16
TOKENS = 8192
N_TP = 2


def draw_cache_lens(key, part):
    key_one, key_two, key_three, key_four = jax.random.split(jax.random.fold_in(key, 11), 4)
    factor_one = jax.random.randint(key_one, (REQS,), 0, CACHE + 1)
    factor_two = jax.random.randint(key_two, (REQS,), 0, CACHE + 1)
    lengths = factor_one * factor_two // CACHE
    longest = jax.random.randint(key_three, (), 0, REQS)
    offset = jax.random.randint(key_four, (), 1, REQS)
    emptied = (longest + offset) % REQS
    request_ids = jnp.arange(REQS)
    lengths = jnp.where(request_ids == longest, CACHE, lengths)
    lengths = jnp.where(request_ids == emptied, 0, lengths)
    return lengths.astype(jnp.int32)


def draw_valid_tokens(key, part):
    key_one, key_two = jax.random.split(jax.random.fold_in(key, 23), 2)
    counts = jax.random.randint(key_one, (REQS,), SPAN // 4, SPAN + 1)
    fullest = jax.random.randint(key_two, (), 0, REQS)
    counts = jnp.where(jnp.arange(REQS) == fullest, SPAN, counts)
    return counts.astype(jnp.int32)


def draw_cache(key, part):
    key_one = jax.random.fold_in(jax.random.fold_in(key, 37), 0)
    entries = jnp.clip(jax.random.normal(key_one, (REQS, 2, CACHE, HEADS * HD), jnp.float32), -6.0, 6.0)
    return entries.astype(jnp.bfloat16)


def spiked(values, key, source, target, shards_of, factor):
    def block_of(axis_at):
        return (jnp.arange(values.shape[axis_at]) // (values.shape[axis_at] // shards_of)).reshape((-1,) + (1,) * (values.ndim - 1 - axis_at))

    one_side = jax.random.permutation(key, shards_of)[block_of(target)]
    second = (block_of(target) + shards_of // 2) % shards_of
    return jnp.where((block_of(source) == one_side) | (block_of(source) == second), factor * values, values)


def block_scale(stream_key, extent, pieces, smallest, high):
    gain = 1.0
    for dim, blocks in pieces:
        heights = jax.random.uniform(jax.random.fold_in(jax.random.fold_in(stream_key, 6), dim), (blocks,), jnp.float32, smallest / len(pieces), high / len(pieces))
        gain = gain * jnp.repeat(jnp.exp(heights), extent[dim] // blocks).reshape((-1,) + (1,) * (len(extent) - 1 - dim))
    return gain


def gaussian(rng, shape, width, bound, cuts=(), held_as=jnp.bfloat16):
    factor_of = block_scale(rng, shape, cuts, -0.22, 0.18) if cuts else 1.0
    array = jax.random.normal(rng, shape, jnp.float32) * width * factor_of
    return jnp.minimum(jnp.maximum(array, -bound), bound).astype(held_as)


def noise_with(stream_key, extent, deviation, most, pieces, heavy, kind=jnp.bfloat16):
    values = deviation * jax.random.normal(stream_key, extent, jnp.float32)
    if pieces:
        values = values * block_scale(stream_key, extent, pieces, -0.22, 0.18)
    return jnp.clip(spiked(values, jax.random.fold_in(stream_key, 3), *heavy), -most, most).astype(kind)


def setup_inputs(seed: int = 0) -> dict:
    seeds = jax.random.split(jax.random.key(seed), 8)
    return {
        "tokens": gaussian(seeds[0], (TOKENS, D), 1.0, 6.0, ((0, 16), (1, 2))),
        "norm_gain": jnp.clip(1.0 + 0.18 * jax.random.normal(seeds[1], (D,), jnp.float32), 0.099609375, 1.8984375).astype(jnp.bfloat16),
        "qkv_weight": gaussian(seeds[2], (3, D, HEADS * HD), D ** -0.5, 0.109375, ((1, 16), (2, 2))),
        "out_weight": noise_with(seeds[3], (HEADS * HD, D), (HD // 4) ** -0.5, 1.75, ((0, 2), (1, 16)), (0, 1, 16, 2.0)),
        "cache": draw_cache(jax.random.fold_in(seeds[7], 71), 0),
        "cache_lens": draw_cache_lens(jax.random.fold_in(seeds[7], 71), 0),
        "valid_tokens": draw_valid_tokens(jax.random.fold_in(seeds[7], 71), 0),
    }


epsilon = 1e-05
masked_value = -1e+30
theta_base = 10000.0

def rotate(projected, positions):
    tokens_here, columns = projected.shape
    per_head = projected.reshape(tokens_here, columns // HD, HD)
    frequencies = jnp.power(theta_base, -jnp.arange(0, HD, 2, dtype=jnp.float32) / HD)
    angles = positions.astype(jnp.float32)[:, None] * frequencies[None, :]
    cosine = jnp.cos(angles)[:, None, :]
    sine_table = jnp.sin(angles)[:, None, :]
    first_half = per_head[..., :HD // 2]
    second_half = per_head[..., HD // 2:]
    turned = jnp.concatenate([first_half * cosine - second_half * sine_table, second_half * cosine + first_half * sine_table], axis=-1)
    return turned.reshape(tokens_here, columns)

def reference(tokens, norm_gain, qkv_weight, out_weight, cache, cache_lens, valid_tokens):
    head_cols = HEADS * HD
    group_cols = head_cols // N_TP
    score_scale = 1.0 / math.sqrt(HD)
    rows_all = tokens.reshape(REQS, SPAN, D)

    def per_request(inputs_all):
        rows_in, cache_here, length, valid_count = inputs_all
        inputs = rows_in.astype(jnp.float32)
        spread = lax.optimization_barrier(jnp.mean(inputs * inputs, axis=-1, keepdims=True))
        normed = (inputs * lax.rsqrt(spread + epsilon) * norm_gain.astype(jnp.float32)).astype(jnp.bfloat16)
        projected = [jnp.dot(normed, qkv_weight[j], preferred_element_type=jnp.float32) for j in range(3)]
        token_ids = jnp.arange(SPAN, dtype=jnp.int32)
        positions = length + token_ids
        queries = rotate(projected[0], positions).astype(jnp.bfloat16)
        keys_new = rotate(projected[1], positions).astype(jnp.bfloat16)
        values_new = projected[2].astype(jnp.bfloat16)
        kept = (token_ids < valid_count)[:, None]
        entries = jnp.stack([jnp.where(kept, keys_new, jnp.zeros_like(keys_new)), jnp.where(kept, values_new, jnp.zeros_like(values_new))])
        key_rows = jnp.concatenate([cache_here[0], keys_new], axis=0)
        value_rows = jnp.concatenate([cache_here[1], values_new], axis=0)
        cache_ids = jnp.arange(CACHE, dtype=jnp.int32)
        cache_mask = jnp.broadcast_to((cache_ids < length)[None, :], (SPAN, CACHE))
        new_mask = (token_ids[None, :] <= token_ids[:, None]) & (token_ids[None, :] < valid_count)
        live_mask = jnp.concatenate([cache_mask, new_mask], axis=1)
        scores = jnp.einsum('thd,shd->hts', queries.reshape(SPAN, HEADS, HD).astype(jnp.float32), key_rows.reshape(CACHE + SPAN, HEADS, HD).astype(jnp.float32)) * score_scale
        scores = jnp.where(live_mask[None], scores, masked_value)
        maximum = lax.optimization_barrier(jnp.max(scores, axis=-1, keepdims=True))
        expo = jnp.exp(scores - maximum)
        weights = (expo / lax.optimization_barrier(jnp.sum(expo, axis=-1, keepdims=True))).astype(jnp.bfloat16)
        attended = jnp.einsum('hts,shd->thd', weights.astype(jnp.float32), value_rows.reshape(CACHE + SPAN, HEADS, HD).astype(jnp.float32))
        attended = attended.astype(jnp.bfloat16).reshape(SPAN, head_cols)
        partial_value = jnp.einsum('tgc,gcd->gtd', attended.reshape(SPAN, N_TP, group_cols).astype(jnp.float32), out_weight.reshape(N_TP, group_cols, D).astype(jnp.float32))
        partial_value = partial_value.astype(jnp.bfloat16).astype(jnp.float32)
        summed = lax.optimization_barrier(jnp.sum(partial_value, axis=0))
        mixed_rows = jnp.where(kept, summed, jnp.zeros_like(summed)).astype(jnp.bfloat16)
        return (mixed_rows, entries)
    mixed_all, entries_all = lax.map(per_request, (rows_all, cache, cache_lens, valid_tokens))
    return (mixed_all.reshape(TOKENS, D), entries_all)
```

```python
import functools
import math

import jax
import jax.numpy as jnp
from jax import lax
from jax.experimental import pallas as pl
from jax.experimental.pallas import tpu as pltpu
from jax.sharding import PartitionSpec as P

HD = 96
GROUP = 4 * HD

epsilon = 1e-05
masked_value = -1e30
theta_base = 10000.0


def rope_tables(positions):
    frequencies = jnp.power(theta_base, -jnp.arange(0, HD, 2, dtype=jnp.float32) / HD)
    angles = positions.astype(jnp.float32)[:, None] * jnp.tile(frequencies, 2)[None, :]
    sign = jnp.where(jnp.arange(HD) < HD // 2, -1.0, 1.0).astype(jnp.float32)
    return (
        jnp.tile(jnp.cos(angles), (1, GROUP // HD)),
        jnp.tile(jnp.sin(angles) * sign[None, :], (1, GROUP // HD)),
    )


def attend_kernel(span, cached, block, limits, proj, cos_ref, sin_ref, cache, att, entries, q_s):
    length = limits[0]
    valid = limits[1]
    cosine = cos_ref[...]
    sine = sin_ref[...]
    first = lax.broadcasted_iota(jnp.int32, (span, GROUP), 1) % HD < HD // 2

    def rotate(v):
        ahead = pltpu.roll(v, GROUP - HD // 2, 1)
        behind = pltpu.roll(v, HD // 2, 1)
        return v * cosine + jnp.where(first, ahead, behind) * sine

    q_s[0] = rotate(proj[0]).astype(jnp.bfloat16)
    q_s[1] = rotate(proj[1]).astype(jnp.bfloat16)
    q_s[2] = proj[2].astype(jnp.bfloat16)
    kept = lax.broadcasted_iota(jnp.int32, (span, GROUP), 0) < valid
    zeros = jnp.zeros((span, GROUP), jnp.float32)
    entries[0, 0] = jnp.where(kept, q_s[1].astype(jnp.float32), zeros).astype(jnp.bfloat16)
    entries[0, 1] = jnp.where(kept, q_s[2].astype(jnp.float32), zeros).astype(jnp.bfloat16)

    scale = math.log2(math.e) / math.sqrt(HD)
    cache_bias = jnp.where(
        lax.broadcasted_iota(jnp.int32, (1, cached), 1) < length, 0.0, masked_value
    )
    dims = (((1,), (1,)), ((), ()))
    for step in range(span // block):
        rows = slice(step * block, (step + 1) * block)
        seen = (step + 1) * block
        row_ids = lax.broadcasted_iota(jnp.int32, (block, seen), 0) + step * block
        col_ids = lax.broadcasted_iota(jnp.int32, (block, seen), 1)
        live = (col_ids <= row_ids) & (col_ids < valid)
        gathered = [None] * (GROUP // 128)
        for head in range(GROUP // HD):
            low = head * HD // 128 * 128
            high = -(-(head + 1) * HD // 128) * 128
            window = slice(low, high)
            lane = lax.broadcasted_iota(jnp.int32, (block, high - low), 1) + low
            mine = (lane >= head * HD) & (lane < (head + 1) * HD)
            query = jnp.where(mine, q_s[0, rows, window].astype(jnp.float32), 0.0).astype(
                jnp.bfloat16
            )
            old = (
                lax.dot_general(
                    query, cache[0, 0, :, window], dims, preferred_element_type=jnp.float32
                )
                * scale
                + cache_bias
            )
            new = (
                lax.dot_general(
                    query, q_s[1, :seen, window], dims, preferred_element_type=jnp.float32
                )
                * scale
            )
            new = jnp.where(live, new, masked_value)
            top = jnp.maximum(
                jnp.max(old, axis=1, keepdims=True), jnp.max(new, axis=1, keepdims=True)
            )
            old = jnp.exp2(old - top)
            new = jnp.exp2(new - top)
            total = jnp.sum(old, axis=1, keepdims=True) + jnp.sum(new, axis=1, keepdims=True)
            inverse = 1.0 / total
            result = jnp.dot(
                (old * inverse).astype(jnp.bfloat16),
                cache[0, 1, :, window],
                preferred_element_type=jnp.float32,
            ) + jnp.dot(
                (new * inverse).astype(jnp.bfloat16),
                q_s[2, :seen, window],
                preferred_element_type=jnp.float32,
            )
            result = jnp.where(mine, result, 0.0)
            for tile in range(low // 128, high // 128):
                piece = result[:, tile * 128 - low : (tile + 1) * 128 - low]
                gathered[tile] = piece if gathered[tile] is None else gathered[tile] + piece
        for tile, piece in enumerate(gathered):
            att[rows, tile * 128 : (tile + 1) * 128] = piece.astype(jnp.bfloat16)


def attend(limits, projected, cosine, sine, cache):
    _, span, cols = projected.shape
    cached = cache.shape[2]
    block = min(256, span)
    return pl.pallas_call(
        functools.partial(attend_kernel, span, cached, block),
        out_shape=(
            jax.ShapeDtypeStruct((span, cols), jnp.bfloat16),
            jax.ShapeDtypeStruct((1, 2, span, cols), jnp.bfloat16),
        ),
        grid_spec=pltpu.PrefetchScalarGridSpec(
            num_scalar_prefetch=1,
            grid=(cols // GROUP,),
            in_specs=[
                pl.BlockSpec((3, span, GROUP), lambda i, s: (0, 0, i)),
                pl.BlockSpec((span, GROUP), lambda i, s: (0, 0)),
                pl.BlockSpec((span, GROUP), lambda i, s: (0, 0)),
                pl.BlockSpec((1, 2, cached, GROUP), lambda i, s: (0, 0, 0, i)),
            ],
            out_specs=(
                pl.BlockSpec((span, GROUP), lambda i, s: (0, i)),
                pl.BlockSpec((1, 2, span, GROUP), lambda i, s: (0, 0, 0, i)),
            ),
            scratch_shapes=[pltpu.VMEM((3, span, GROUP), jnp.bfloat16)],
        ),
        compiler_params=pltpu.CompilerParams(vmem_limit_bytes=48 << 20),
        cost_estimate=pl.CostEstimate(
            flops=span * (cached + span) * cols * 8,
            bytes_accessed=cached * cols * 4 + span * cols * 20,
            transcendentals=span * (cached + span) * cols // HD,
        ),
        name="attend",
    )(limits, projected, cosine, sine, cache)


def gather_weights(mesh, qkv_weight):
    return lax.all_gather(qkv_weight, "req", axis=1, tiled=True)


def per_device(mesh, tokens, norm_gain, qkv_weight, out_weight, cache, cache_lens, valid_tokens):
    weights = gather_weights(mesh, qkv_weight)
    gathered, gain_all = (
        lax.all_gather(tokens, "tp", axis=1, tiled=True),
        lax.all_gather(norm_gain, "tp", axis=0, tiled=True),
    )
    inputs = gathered.astype(jnp.float32)
    spread = jnp.mean(inputs * inputs, axis=-1, keepdims=True)
    normed = (inputs * lax.rsqrt(spread + epsilon) * gain_all.astype(jnp.float32)).astype(
        jnp.bfloat16
    )
    token_ids = jnp.arange(normed.shape[0], dtype=jnp.int32)
    cosine, sine = rope_tables(cache_lens[0] + token_ids)
    projected = jnp.einsum("td,jdc->jtc", normed, weights, preferred_element_type=jnp.float32)
    turned, _ = lax.optimization_barrier((out_weight.T, weights[0, :8, :128]))
    out_all = lax.all_gather(turned, "req", axis=0, tiled=True)
    limits = jnp.concatenate([cache_lens, valid_tokens])
    attended, new_entries = attend(limits, projected, cosine, sine, cache)
    partial_value = lax.dot_general(
        attended, out_all, (((1,), (1,)), ((), ())), preferred_element_type=jnp.float32
    )
    summed = lax.psum_scatter(
        partial_value.astype(jnp.bfloat16), "tp", scatter_dimension=1, tiled=True
    ).astype(jnp.float32)
    kept = (token_ids < valid_tokens[0])[:, None]
    mixed_out = jnp.where(kept, summed, jnp.zeros_like(summed)).astype(jnp.bfloat16)
    return (mixed_out, new_entries)


def solution(mesh):
    placed = (
        P("req", "tp"),
        P("tp"),
        P(None, "req", "tp"),
        P("tp", "req"),
        P("req", None, None, "tp"),
        P("req"),
        P("req"),
    )
    return jax.shard_map(
        functools.partial(per_device, mesh),
        mesh=mesh,
        in_specs=placed,
        out_specs=(P("req", "tp"), P("req", None, None, "tp")),
        check_vma=False,
    )
```

```python
import functools
import math

import jax
import jax.numpy as jnp
from jax import lax
from jax.experimental import pallas as pl
from jax.experimental.pallas import tpu as pltpu
from jax.sharding import PartitionSpec as P

HD = 96
GROUP = 4 * HD

epsilon = 1e-05
masked_value = -1e30
theta_base = 10000.0


def rope_tables(positions):
    frequencies = jnp.power(theta_base, -jnp.arange(0, HD, 2, dtype=jnp.float32) / HD)
    angles = positions.astype(jnp.float32)[:, None] * jnp.tile(frequencies, 2)[None, :]
    sign = jnp.where(jnp.arange(HD) < HD // 2, -1.0, 1.0).astype(jnp.float32)
    return (
        jnp.tile(jnp.cos(angles), (1, GROUP // HD)),
        jnp.tile(jnp.sin(angles) * sign[None, :], (1, GROUP // HD)),
    )


def attend_kernel(span, cached, block, limits, proj, cos_ref, sin_ref, cache, att, entries, q_s):
    length = limits[0]
    valid = limits[1]
    cosine = cos_ref[...]
    sine = sin_ref[...]
    first = lax.broadcasted_iota(jnp.int32, (span, GROUP), 1) % HD < HD // 2

    def rotate(v):
        ahead = pltpu.roll(v, GROUP - HD // 2, 1)
        behind = pltpu.roll(v, HD // 2, 1)
        return v * cosine + jnp.where(first, ahead, behind) * sine

    q_s[0] = rotate(proj[0]).astype(jnp.bfloat16)
    q_s[1] = rotate(proj[1]).astype(jnp.bfloat16)
    q_s[2] = proj[2].astype(jnp.bfloat16)
    kept = lax.broadcasted_iota(jnp.int32, (span, GROUP), 0) < valid
    zeros = jnp.zeros((span, GROUP), jnp.float32)
    entries[0, 0] = jnp.where(kept, q_s[1].astype(jnp.float32), zeros).astype(jnp.bfloat16)
    entries[0, 1] = jnp.where(kept, q_s[2].astype(jnp.float32), zeros).astype(jnp.bfloat16)

    scale = math.log2(math.e) / math.sqrt(HD)
    cache_bias = jnp.where(
        lax.broadcasted_iota(jnp.int32, (1, cached), 1) < length, 0.0, masked_value
    )
    dims = (((1,), (1,)), ((), ()))
    for step in range(span // block):
        rows = slice(step * block, (step + 1) * block)
        seen = (step + 1) * block
        row_ids = lax.broadcasted_iota(jnp.int32, (block, seen), 0) + step * block
        col_ids = lax.broadcasted_iota(jnp.int32, (block, seen), 1)
        live = (col_ids <= row_ids) & (col_ids < valid)
        gathered = [None] * (GROUP // 128)
        for head in range(GROUP // HD):
            low = head * HD // 128 * 128
            high = -(-(head + 1) * HD // 128) * 128
            window = slice(low, high)
            lane = lax.broadcasted_iota(jnp.int32, (block, high - low), 1) + low
            mine = (lane >= head * HD) & (lane < (head + 1) * HD)
            query = jnp.where(mine, q_s[0, rows, window].astype(jnp.float32), 0.0).astype(
                jnp.bfloat16
            )
            old = (
                lax.dot_general(
                    query, cache[0, 0, :, window], dims, preferred_element_type=jnp.float32
                )
                * scale
                + cache_bias
            )
            new = (
                lax.dot_general(
                    query, q_s[1, :seen, window], dims, preferred_element_type=jnp.float32
                )
                * scale
            )
            new = jnp.where(live, new, masked_value)
            top = jnp.maximum(
                jnp.max(old, axis=1, keepdims=True), jnp.max(new, axis=1, keepdims=True)
            )
            old = jnp.exp2(old - top)
            new = jnp.exp2(new - top)
            total = jnp.sum(old, axis=1, keepdims=True) + jnp.sum(new, axis=1, keepdims=True)
            inverse = 1.0 / total
            result = jnp.dot(
                (old * inverse).astype(jnp.bfloat16),
                cache[0, 1, :, window],
                preferred_element_type=jnp.float32,
            ) + jnp.dot(
                (new * inverse).astype(jnp.bfloat16),
                q_s[2, :seen, window],
                preferred_element_type=jnp.float32,
            )
            result = jnp.where(mine, result, 0.0)
            for tile in range(low // 128, high // 128):
                piece = result[:, tile * 128 - low : (tile + 1) * 128 - low]
                gathered[tile] = piece if gathered[tile] is None else gathered[tile] + piece
        for tile, piece in enumerate(gathered):
            att[rows, tile * 128 : (tile + 1) * 128] = piece.astype(jnp.bfloat16)


def attend(limits, projected, cosine, sine, cache):
    _, span, cols = projected.shape
    cached = cache.shape[2]
    block = min(256, span)
    return pl.pallas_call(
        functools.partial(attend_kernel, span, cached, block),
        out_shape=(
            jax.ShapeDtypeStruct((span, cols), jnp.bfloat16),
            jax.ShapeDtypeStruct((1, 2, span, cols), jnp.bfloat16),
        ),
        grid_spec=pltpu.PrefetchScalarGridSpec(
            num_scalar_prefetch=1,
            grid=(cols // GROUP,),
            in_specs=[
                pl.BlockSpec((3, span, GROUP), lambda i, s: (0, 0, i)),
                pl.BlockSpec((span, GROUP), lambda i, s: (0, 0)),
                pl.BlockSpec((span, GROUP), lambda i, s: (0, 0)),
                pl.BlockSpec((1, 2, cached, GROUP), lambda i, s: (0, 0, 0, i)),
            ],
            out_specs=(
                pl.BlockSpec((span, GROUP), lambda i, s: (0, i)),
                pl.BlockSpec((1, 2, span, GROUP), lambda i, s: (0, 0, 0, i)),
            ),
            scratch_shapes=[pltpu.VMEM((3, span, GROUP), jnp.bfloat16)],
        ),
        compiler_params=pltpu.CompilerParams(vmem_limit_bytes=48 << 20),
        cost_estimate=pl.CostEstimate(
            flops=span * (cached + span) * cols * 8,
            bytes_accessed=cached * cols * 4 + span * cols * 20,
            transcendentals=span * (cached + span) * cols // HD,
        ),
        name="attend",
    )(limits, projected, cosine, sine, cache)


def gather_events():
    events = []
    for stream, order in enumerate(("xyz", "zyx", "zxy")):
        for dz in range(-3, 4):
            for dy in range(2):
                for dx in range(2):
                    offset = {"z": dz, "y": dy, "x": dx}
                    moved = [axis for axis in order if offset[axis]]
                    if moved:
                        hops = abs(dz) + dy + dx
                        events.append((hops, order.index(moved[-1]), stream, moved[-1], dz, dy, dx))
    events.sort()
    return [(stream, via, dz, dy, dx) for _, _, stream, via, dz, dy, dx in events]


def gather_kernel(cuts, shard, full, send_sem, recv_sem, own_sem):
    me = lax.axis_index("req")
    core = lax.axis_index("tp")
    z, y, x = lax.div(me, 4), lax.rem(lax.div(me, 2), 2), lax.rem(me, 2)
    beside = {"x": me + 1 - 2 * x, "y": me + 2 - 4 * y}
    orders = ("xyz", "zyx", "zxy")

    barrier = pltpu.get_barrier_semaphore()

    def greet(target):
        pl.semaphore_signal(
            barrier, inc=1, device_id=(target, core), device_id_type=pl.DeviceIdType.MESH
        )

    greet(beside["x"])
    greet(beside["y"])

    @pl.when(z < 3)
    def _():
        greet(me + 4)

    @pl.when(z > 0)
    def _():
        greet(me - 4)

    inner = jnp.where(z > 0, 1, 0) + jnp.where(z < 3, 1, 0)
    pl.semaphore_wait(barrier, 2 + inner)

    def block(ref, stream, source):
        return ref.at[:, source, cuts[stream] : cuts[stream + 1], :]

    def copy(stream, source, lane, target, own):
        there = block(full, stream, source)
        here = shard.at[:, cuts[stream] : cuts[stream + 1], :] if own else there
        return pltpu.make_async_remote_copy(
            src_ref=here,
            dst_ref=there,
            send_sem=send_sem.at[stream, source, lane],
            recv_sem=recv_sem.at[stream, source],
            device_id=(target, core),
            device_id_type=pl.DeviceIdType.MESH,
        )

    def forward(stream, source, via, dz, own, act):
        order = orders[stream]
        for axis in order[order.index(via) if via else 0 :]:
            if axis == "z":
                if not via or dz < 0 or via != "z":

                    @pl.when(z < 3)
                    def _():
                        act(copy(stream, source, 0, me + 4, own))

                if not via or dz > 0 or via != "z":

                    @pl.when(z > 0)
                    def _():
                        act(copy(stream, source, 1, me - 4, own))

            elif axis != via:
                lane = 2 if axis == "y" else 3
                act(copy(stream, source, lane, beside[axis], own))

    for stream in (1, 2, 0):
        forward(stream, me, None, 0, True, lambda c: c.start())
    kept = pltpu.make_async_copy(shard, full.at[:, me], own_sem)
    kept.start()

    def visit(event, act, arrived):
        stream, via, dz, dy, dx = event
        source = me + 4 * dz + dy * (2 - 4 * y) + dx * (1 - 2 * x)

        def body():
            if arrived:
                copy(stream, source, 0, beside["x"], False).wait_recv()
            forward(stream, source, via, dz, False, act)

        if dz > 0:
            pl.when(z + dz <= 3)(body)
        elif dz < 0:
            pl.when(z + dz >= 0)(body)
        else:
            body()

    for event in gather_events():
        visit(event, lambda c: c.start(), True)
    for stream in (1, 2, 0):
        forward(stream, me, None, 0, True, lambda c: c.wait_send())
    for event in gather_events():
        visit(event, lambda c: c.wait_send(), False)
    kept.wait()


def gather_weights(mesh, shard):
    peers = mesh.shape["req"]
    count, rows, cols = shard.shape
    if peers != 16 or rows % 192:
        return lax.all_gather(shard, "req", axis=1, tiled=True)
    unit = rows // 12
    cuts = (0, 2 * unit, 7 * unit, rows)
    full = pl.pallas_call(
        functools.partial(gather_kernel, cuts),
        out_shape=jax.ShapeDtypeStruct((count, peers, rows, cols), shard.dtype),
        in_specs=[pl.BlockSpec(memory_space=pl.ANY)],
        out_specs=pl.BlockSpec(memory_space=pl.ANY),
        scratch_shapes=[
            pltpu.SemaphoreType.DMA((3, peers, 4)),
            pltpu.SemaphoreType.DMA((3, peers)),
            pltpu.SemaphoreType.DMA,
        ],
        compiler_params=pltpu.CompilerParams(collective_id=0, has_side_effects=True),
        name="gather_weights",
    )(shard)
    return full.reshape(count, peers * rows, cols)


def per_device(mesh, tokens, norm_gain, qkv_weight, out_weight, cache, cache_lens, valid_tokens):
    weights = gather_weights(mesh, qkv_weight)
    gathered, gain_all = (
        lax.all_gather(tokens, "tp", axis=1, tiled=True),
        lax.all_gather(norm_gain, "tp", axis=0, tiled=True),
    )
    inputs = gathered.astype(jnp.float32)
    spread = jnp.mean(inputs * inputs, axis=-1, keepdims=True)
    normed = (inputs * lax.rsqrt(spread + epsilon) * gain_all.astype(jnp.float32)).astype(
        jnp.bfloat16
    )
    token_ids = jnp.arange(normed.shape[0], dtype=jnp.int32)
    cosine, sine = rope_tables(cache_lens[0] + token_ids)
    projected = jnp.einsum("td,jdc->jtc", normed, weights, preferred_element_type=jnp.float32)
    turned, _ = lax.optimization_barrier((out_weight.T, weights[0, :8, :128]))
    out_all = lax.all_gather(turned, "req", axis=0, tiled=True)
    limits = jnp.concatenate([cache_lens, valid_tokens])
    attended, new_entries = attend(limits, projected, cosine, sine, cache)
    partial_value = lax.dot_general(
        attended, out_all, (((1,), (1,)), ((), ())), preferred_element_type=jnp.float32
    )
    summed = lax.psum_scatter(
        partial_value.astype(jnp.bfloat16), "tp", scatter_dimension=1, tiled=True
    ).astype(jnp.float32)
    kept = (token_ids < valid_tokens[0])[:, None]
    mixed_out = jnp.where(kept, summed, jnp.zeros_like(summed)).astype(jnp.bfloat16)
    return (mixed_out, new_entries)


def solution(mesh):
    placed = (
        P("req", "tp"),
        P("tp"),
        P(None, "req", "tp"),
        P("tp", "req"),
        P("req", None, None, "tp"),
        P("req"),
        P("req"),
    )
    return jax.shard_map(
        functools.partial(per_device, mesh),
        mesh=mesh,
        in_specs=placed,
        out_specs=(P("req", "tp"), P("req", None, None, "tp")),
        check_vma=False,
    )
```

```python
import functools
import math

import jax
import jax.numpy as jnp
from jax import lax
from jax.experimental import pallas as pl
from jax.experimental.pallas import tpu as pltpu
from jax.sharding import PartitionSpec as P

HD = 96
GROUP = 4 * HD

epsilon = 1e-05
masked_value = -1e30
theta_base = 10000.0


def rope_tables(positions):
    frequencies = jnp.power(theta_base, -jnp.arange(0, HD, 2, dtype=jnp.float32) / HD)
    angles = positions.astype(jnp.float32)[:, None] * jnp.tile(frequencies, 2)[None, :]
    sign = jnp.where(jnp.arange(HD) < HD // 2, -1.0, 1.0).astype(jnp.float32)
    return (
        jnp.tile(jnp.cos(angles), (1, GROUP // HD)),
        jnp.tile(jnp.sin(angles) * sign[None, :], (1, GROUP // HD)),
    )


def attend_kernel(span, cached, block, limits, proj, cos_ref, sin_ref, cache, att, entries, q_s):
    length = limits[0]
    valid = limits[1]
    cosine = cos_ref[...]
    sine = sin_ref[...]
    first = lax.broadcasted_iota(jnp.int32, (span, GROUP), 1) % HD < HD // 2

    def rotate(v):
        ahead = pltpu.roll(v, GROUP - HD // 2, 1)
        behind = pltpu.roll(v, HD // 2, 1)
        return v * cosine + jnp.where(first, ahead, behind) * sine

    q_s[0] = rotate(proj[0]).astype(jnp.bfloat16)
    q_s[1] = rotate(proj[1]).astype(jnp.bfloat16)
    q_s[2] = proj[2].astype(jnp.bfloat16)
    kept = lax.broadcasted_iota(jnp.int32, (span, GROUP), 0) < valid
    zeros = jnp.zeros((span, GROUP), jnp.float32)
    entries[0, 0] = jnp.where(kept, q_s[1].astype(jnp.float32), zeros).astype(jnp.bfloat16)
    entries[0, 1] = jnp.where(kept, q_s[2].astype(jnp.float32), zeros).astype(jnp.bfloat16)

    scale = math.log2(math.e) / math.sqrt(HD)
    cache_bias = jnp.where(
        lax.broadcasted_iota(jnp.int32, (1, cached), 1) < length, 0.0, masked_value
    )
    dims = (((1,), (1,)), ((), ()))
    for step in range(span // block):
        rows = slice(step * block, (step + 1) * block)
        seen = (step + 1) * block
        row_ids = lax.broadcasted_iota(jnp.int32, (block, seen), 0) + step * block
        col_ids = lax.broadcasted_iota(jnp.int32, (block, seen), 1)
        live = (col_ids <= row_ids) & (col_ids < valid)
        gathered = [None] * (GROUP // 128)
        for head in range(GROUP // HD):
            low = head * HD // 128 * 128
            high = -(-(head + 1) * HD // 128) * 128
            window = slice(low, high)
            lane = lax.broadcasted_iota(jnp.int32, (block, high - low), 1) + low
            mine = (lane >= head * HD) & (lane < (head + 1) * HD)
            query = jnp.where(mine, q_s[0, rows, window].astype(jnp.float32), 0.0).astype(
                jnp.bfloat16
            )
            old = (
                lax.dot_general(
                    query, cache[0, 0, :, window], dims, preferred_element_type=jnp.float32
                )
                * scale
                + cache_bias
            )
            new = (
                lax.dot_general(
                    query, q_s[1, :seen, window], dims, preferred_element_type=jnp.float32
                )
                * scale
            )
            new = jnp.where(live, new, masked_value)
            top = jnp.maximum(
                jnp.max(old, axis=1, keepdims=True), jnp.max(new, axis=1, keepdims=True)
            )
            old = jnp.exp2(old - top)
            new = jnp.exp2(new - top)
            total = jnp.sum(old, axis=1, keepdims=True) + jnp.sum(new, axis=1, keepdims=True)
            inverse = 1.0 / total
            result = jnp.dot(
                (old * inverse).astype(jnp.bfloat16),
                cache[0, 1, :, window],
                preferred_element_type=jnp.float32,
            ) + jnp.dot(
                (new * inverse).astype(jnp.bfloat16),
                q_s[2, :seen, window],
                preferred_element_type=jnp.float32,
            )
            result = jnp.where(mine, result, 0.0)
            for tile in range(low // 128, high // 128):
                piece = result[:, tile * 128 - low : (tile + 1) * 128 - low]
                gathered[tile] = piece if gathered[tile] is None else gathered[tile] + piece
        for tile, piece in enumerate(gathered):
            att[rows, tile * 128 : (tile + 1) * 128] = piece.astype(jnp.bfloat16)


def attend(limits, projected, cosine, sine, cache):
    _, span, cols = projected.shape
    cached = cache.shape[2]
    block = min(256, span)
    return pl.pallas_call(
        functools.partial(attend_kernel, span, cached, block),
        out_shape=(
            jax.ShapeDtypeStruct((span, cols), jnp.bfloat16),
            jax.ShapeDtypeStruct((1, 2, span, cols), jnp.bfloat16),
        ),
        grid_spec=pltpu.PrefetchScalarGridSpec(
            num_scalar_prefetch=1,
            grid=(cols // GROUP,),
            in_specs=[
                pl.BlockSpec((3, span, GROUP), lambda i, s: (0, 0, i)),
                pl.BlockSpec((span, GROUP), lambda i, s: (0, 0)),
                pl.BlockSpec((span, GROUP), lambda i, s: (0, 0)),
                pl.BlockSpec((1, 2, cached, GROUP), lambda i, s: (0, 0, 0, i)),
            ],
            out_specs=(
                pl.BlockSpec((span, GROUP), lambda i, s: (0, i)),
                pl.BlockSpec((1, 2, span, GROUP), lambda i, s: (0, 0, 0, i)),
            ),
            scratch_shapes=[pltpu.VMEM((3, span, GROUP), jnp.bfloat16)],
        ),
        compiler_params=pltpu.CompilerParams(vmem_limit_bytes=48 << 20),
        cost_estimate=pl.CostEstimate(
            flops=span * (cached + span) * cols * 8,
            bytes_accessed=cached * cols * 4 + span * cols * 20,
            transcendentals=span * (cached + span) * cols // HD,
        ),
        name="attend",
    )(limits, projected, cosine, sine, cache)


def gather_events():
    events = []
    for stream, order in enumerate(("xyz", "zyx", "zxy")):
        for dz in range(-3, 4):
            for dy in range(2):
                for dx in range(2):
                    offset = {"z": dz, "y": dy, "x": dx}
                    moved = [axis for axis in order if offset[axis]]
                    if moved:
                        hops = abs(dz) + dy + dx
                        events.append((hops, order.index(moved[-1]), stream, moved[-1], dz, dy, dx))
    events.sort()
    return [(stream, via, dz, dy, dx) for _, _, stream, via, dz, dy, dx in events]


def gather_kernel(cuts, shard, later, full, released, send_sem, recv_sem, own_sem, later_sem):
    me = lax.axis_index("req")
    core = lax.axis_index("tp")
    z, y, x = lax.div(me, 4), lax.rem(lax.div(me, 2), 2), lax.rem(me, 2)
    beside = {"x": me + 1 - 2 * x, "y": me + 2 - 4 * y}
    orders = ("xyz", "zyx", "zxy")

    barrier = pltpu.get_barrier_semaphore()

    def greet(target):
        pl.semaphore_signal(
            barrier, inc=1, device_id=(target, core), device_id_type=pl.DeviceIdType.MESH
        )

    greet(beside["x"])
    greet(beside["y"])

    @pl.when(z < 3)
    def _():
        greet(me + 4)

    @pl.when(z > 0)
    def _():
        greet(me - 4)

    inner = jnp.where(z > 0, 1, 0) + jnp.where(z < 3, 1, 0)
    pl.semaphore_wait(barrier, 2 + inner)

    def block(ref, stream, source):
        return ref.at[:, source, cuts[stream] : cuts[stream + 1], :]

    def copy(stream, source, lane, target, own):
        there = block(full, stream, source)
        here = shard.at[:, cuts[stream] : cuts[stream + 1], :] if own else there
        return pltpu.make_async_remote_copy(
            src_ref=here,
            dst_ref=there,
            send_sem=send_sem.at[stream, source, lane],
            recv_sem=recv_sem.at[stream, source],
            device_id=(target, core),
            device_id_type=pl.DeviceIdType.MESH,
        )

    def forward(stream, source, via, dz, own, act):
        order = orders[stream]
        for axis in order[order.index(via) if via else 0 :]:
            if axis == "z":
                if not via or dz < 0 or via != "z":

                    @pl.when(z < 3)
                    def _():
                        act(copy(stream, source, 0, me + 4, own))

                if not via or dz > 0 or via != "z":

                    @pl.when(z > 0)
                    def _():
                        act(copy(stream, source, 1, me - 4, own))

            elif axis != via:
                lane = 2 if axis == "y" else 3
                act(copy(stream, source, lane, beside[axis], own))

    for stream in (1, 2, 0):
        forward(stream, me, None, 0, True, lambda c: c.start())
    kept = pltpu.make_async_copy(shard, full.at[:, me], own_sem)
    kept.start()
    held = pltpu.make_async_copy(later, released, later_sem)
    held.start()

    def visit(event, act, arrived):
        stream, via, dz, dy, dx = event
        source = me + 4 * dz + dy * (2 - 4 * y) + dx * (1 - 2 * x)

        def body():
            if arrived:
                copy(stream, source, 0, beside["x"], False).wait_recv()
            forward(stream, source, via, dz, False, act)

        if dz > 0:
            pl.when(z + dz <= 3)(body)
        elif dz < 0:
            pl.when(z + dz >= 0)(body)
        else:
            body()

    for event in gather_events():
        visit(event, lambda c: c.start(), True)
    for stream in (1, 2, 0):
        forward(stream, me, None, 0, True, lambda c: c.wait_send())
    for event in gather_events():
        visit(event, lambda c: c.wait_send(), False)
    kept.wait()
    held.wait()


def gather_weights(mesh, shard, later):
    peers = mesh.shape["req"]
    count, rows, cols = shard.shape
    if peers != 16 or rows % 192:
        return lax.all_gather(shard, "req", axis=1, tiled=True), later
    unit = rows // 12
    cuts = (0, 2 * unit, 7 * unit, rows)
    full, released = pl.pallas_call(
        functools.partial(gather_kernel, cuts),
        out_shape=(
            jax.ShapeDtypeStruct((count, peers, rows, cols), shard.dtype),
            jax.ShapeDtypeStruct(later.shape, later.dtype),
        ),
        in_specs=[pl.BlockSpec(memory_space=pl.ANY)] * 2,
        out_specs=(pl.BlockSpec(memory_space=pl.ANY),) * 2,
        scratch_shapes=[
            pltpu.SemaphoreType.DMA((3, peers, 4)),
            pltpu.SemaphoreType.DMA((3, peers)),
            pltpu.SemaphoreType.DMA,
            pltpu.SemaphoreType.DMA,
        ],
        compiler_params=pltpu.CompilerParams(collective_id=0, has_side_effects=True),
        name="gather_weights",
    )(shard, later)
    return full.reshape(count, peers * rows, cols), released


def per_device(mesh, tokens, norm_gain, qkv_weight, out_weight, cache, cache_lens, valid_tokens):
    turned = out_weight.T
    cut = turned.shape[1] * 5 // 12 // 128 * 128
    out_early = lax.all_gather(turned[:, :cut], "req", axis=0, tiled=True)
    weights, released = gather_weights(mesh, qkv_weight, turned[:, cut:])
    out_late = lax.all_gather(released, "req", axis=0, tiled=True)
    gathered, gain_all = (
        lax.all_gather(tokens, "tp", axis=1, tiled=True),
        lax.all_gather(norm_gain, "tp", axis=0, tiled=True),
    )
    inputs = gathered.astype(jnp.float32)
    spread = jnp.mean(inputs * inputs, axis=-1, keepdims=True)
    normed = (inputs * lax.rsqrt(spread + epsilon) * gain_all.astype(jnp.float32)).astype(
        jnp.bfloat16
    )
    token_ids = jnp.arange(normed.shape[0], dtype=jnp.int32)
    cosine, sine = rope_tables(cache_lens[0] + token_ids)
    projected = jnp.einsum("td,jdc->jtc", normed, weights, preferred_element_type=jnp.float32)
    limits = jnp.concatenate([cache_lens, valid_tokens])
    attended, new_entries = attend(limits, projected, cosine, sine, cache)
    rows_dims = (((1,), (1,)), ((), ()))
    partial_value = lax.dot_general(
        attended[:, :cut], out_early, rows_dims, preferred_element_type=jnp.float32
    ) + lax.dot_general(
        attended[:, cut:], out_late, rows_dims, preferred_element_type=jnp.float32
    )
    summed = lax.psum_scatter(
        partial_value.astype(jnp.bfloat16), "tp", scatter_dimension=1, tiled=True
    ).astype(jnp.float32)
    kept = (token_ids < valid_tokens[0])[:, None]
    mixed_out = jnp.where(kept, summed, jnp.zeros_like(summed)).astype(jnp.bfloat16)
    return (mixed_out, new_entries)


def solution(mesh):
    placed = (
        P("req", "tp"),
        P("tp"),
        P(None, "req", "tp"),
        P("tp", "req"),
        P("req", None, None, "tp"),
        P("req"),
        P("req"),
    )
    return jax.shard_map(
        functools.partial(per_device, mesh),
        mesh=mesh,
        in_specs=placed,
        out_specs=(P("req", "tp"), P("req", None, None, "tp")),
        check_vma=False,
    )
```
